32 devices in a mesh: dp: 1, seq: 32 (over z, y, x, core).
Axes of the slice: x: 2, y: 2, z: 4, core: 2. Of those that a mesh axis runs over, the one named last changes fastest.
Arguments:
- queries: bfloat16 [1, 1024, 6144], P('dp', None, 'seq'), may hold values from -360 to 360
- latent: bfloat16 [1, 1024, 576], P('dp', 'seq'), may hold values from -6 to 6
- latent_gain: float32 [512], replicated, may hold values from 0.1 to 1.9
- segments: int32 [1, 1024], P('dp', 'seq'), may hold values from 0 to 7, never falling along the last dimension, each value on 1 to 256 neighbouring positions
- up_weight: bfloat16 [512, 8192], P('dp', 'seq'), may hold values from -0.25 to 0.25
- out_grad: bfloat16 [1, 1024, 4096], P('dp', None, 'seq'), may hold values from -6 to 6
- hess_old: float32 [512, 8192], P('dp', 'seq'), may hold values from 0.01 to 0.3
Outputs:
- attn_out: bfloat16 [1, 1024, 4096], P('dp', None, 'seq')
- hess_new: float32 [512, 8192], P('dp', 'seq')
The draws below stay inside these ranges and needn't reach their ends.
All inputs are finite; a program needn't handle non-finite values.
Results may differ from the reference program's by a relative error of at most 0.0075.
Values may be sent and summed in bfloat16 or wider, within the bound.
A program may use at most 64 MiB of HBM per device.

```python
import math
import jax
import jax.numpy as jnp
import numpy as np
from jax import lax

D_LAT = 512
D_ROPE = 64
D_NOPE = 128
D_VAL = 128
DOCS = 8
HEADS = 32
SEQ_LEN = 1024
BATCH = 1
DOC_MOST = 256


def latent_values(key):
    latent_key = jax.random.fold_in(key, 7)
    full_shape = (BATCH, SEQ_LEN, D_LAT + D_ROPE)
    values = jnp.clip(jax.random.normal(latent_key, full_shape, jnp.float32), -6.0, 6.0)
    return values.astype(jnp.bfloat16).astype(jnp.float32)


def draw_latent(key, part):
    return latent_values(key).astype(jnp.bfloat16)


def draw_queries(key, part):
    query_width = D_NOPE + D_ROPE
    full_shape = (BATCH, SEQ_LEN, HEADS, query_width)
    base_key = jax.random.fold_in(jax.random.fold_in(key, 11), 0)
    values = jnp.clip(jax.random.normal(base_key, full_shape, jnp.float32), -6.0, 6.0)
    return values.reshape(BATCH, SEQ_LEN, HEADS * query_width).astype(jnp.bfloat16)


def shard_levels(key, shape, cuts, smallest, high):
    loudness = 1.0
    for position, blocks in cuts:
        heights = jax.random.uniform(jax.random.fold_in(jax.random.fold_in(key, 6), position), (blocks,), jnp.float32, smallest / len(cuts), high / len(cuts))
        loudness = loudness * jnp.repeat(jnp.exp(heights), shape[position] // blocks).reshape((-1,) + (1,) * (len(shape) - 1 - position))
    return loudness


def length_profile(count, total, limit, lean):
    loads = [(1 << 20) // math.isqrt(rank ** lean) + 1 for rank in range(2, count + 1)]
    rest, holding = total - limit - (count - 1), [1] * (count - 1)
    while rest > 0:
        movable = [i for i in range(count - 1) if holding[i] < limit]
        whole, remaining = sum([loads[i] for i in movable]), rest
        for i in movable:
            addition = min(limit - holding[i], max(1, remaining * loads[i] // whole), rest)
            holding[i] = holding[i] + addition
            rest = rest - addition
    return np.array([limit] + holding)


def ragged(stream_key, count, total, limit, lean):
    if count == 2:
        one = jax.random.randint(stream_key, (), max(1, total - limit), min(limit, total - 1) + 1)
        return jnp.stack([one, total - one])
    lengths = jnp.asarray(length_profile(count, total, limit, lean), jnp.int32)
    twos = (count - 1) // 2
    giver, sink = lengths[1:1 + 2 * twos:2], lengths[2:2 + 2 * twos:2]
    margin = jnp.minimum(giver - 1, limit - sink)
    moved = jax.random.randint(jax.random.fold_in(stream_key, 1), (twos,), 0, 1 << 20) % (margin + 1)
    lengths = lengths.at[1:1 + 2 * twos:2].set(giver - moved).at[2:2 + 2 * twos:2].set(sink + moved)
    return lengths[jax.random.permutation(jax.random.fold_in(stream_key, 2), count)]


def bell_draw(stream_key, extent, scale, bound, pieces=(), kind=jnp.bfloat16):
    array = scale * jax.random.normal(stream_key, extent, jnp.float32)
    if pieces:
        array = array * shard_levels(stream_key, extent, pieces, -0.22, 0.18)
    return jnp.clip(array, -bound, bound).astype(kind)


def setup_inputs(seed: int = 0) -> dict:
    splits = jax.random.split(jax.random.key(seed), 8)
    return {
        "queries": draw_queries(jax.random.fold_in(splits[7], 71), 0),
        "latent": draw_latent(jax.random.fold_in(splits[7], 71), 0),
        "latent_gain": jnp.clip(1.0 + 0.18 * jax.random.normal(splits[2], (D_LAT,), jnp.float32), 0.1, 1.9),
        "segments": jax.vmap(lambda own: jnp.searchsorted(jnp.cumsum(ragged(own, DOCS, SEQ_LEN, DOC_MOST, 1)), jnp.arange(SEQ_LEN), side="right"))(jax.random.split(splits[3], BATCH)).reshape((BATCH, SEQ_LEN)).astype(jnp.int32),
        "up_weight": bell_draw(splits[4], (D_LAT, HEADS * (D_NOPE + D_VAL)), D_LAT ** -0.5, 0.25, ((1, 32),)),
        "out_grad": bell_draw(splits[5], (BATCH, SEQ_LEN, HEADS * D_VAL), 1.0, 6.0, ((2, 32),)),
        "hess_old": jnp.clip(jnp.exp(math.log(0.3) - 3.4011974 * jax.random.uniform(splits[6], (D_LAT, HEADS * (D_NOPE + D_VAL)), jnp.float32) ** shard_levels(splits[6], (D_LAT, HEADS * (D_NOPE + D_VAL)), ((1, 32),), -0.2, 0.2)), 0.01, 0.3),
    }


epsilon = 1e-06
ema_decay = 0.99
rope_base = 10000.0
masked_score = -1e+30

def doc_positions(seg_ids):
    length = seg_ids.shape[0]
    places = jnp.arange(length, dtype=jnp.int32)
    starts_here = jnp.concatenate([jnp.ones((1,), dtype=bool), seg_ids[1:] != seg_ids[:-1]])
    starts = lax.cummax(jnp.where(starts_here, places, jnp.zeros_like(places)), axis=0)
    return places - starts

def rotate_pairs(values_in, positions):
    half_width = values_in.shape[-1] // 2
    steps_up = jnp.arange(half_width, dtype=jnp.float32)
    frequency = rope_base ** (-(2.0 * steps_up) / values_in.shape[-1])
    angles = positions.astype(jnp.float32)[:, None] * frequency[None, :]
    cosine = jnp.cos(angles)
    sine_term = jnp.sin(angles)
    first_half = values_in[:, :half_width]
    second = values_in[:, half_width:]
    return jnp.concatenate([first_half * cosine - second * sine_term, second * cosine + first_half * sine_term], axis=1)

def normalize(latent_rows, latent_gain):
    compressed = latent_rows[:, :D_LAT].astype(jnp.float32)
    spread = lax.optimization_barrier(jnp.mean(compressed * compressed, axis=-1, keepdims=True))
    return (compressed * lax.rsqrt(spread + epsilon) * latent_gain).astype(jnp.bfloat16)

def attend_head(query_head, out_head, normed, key_rope, weight_head, positions, allowed):
    score_scale = (D_NOPE + D_ROPE) ** (-0.5)
    q_nope = query_head[:, :D_NOPE]
    q_rope = rotate_pairs(query_head[:, D_NOPE:].astype(jnp.float32), positions).astype(jnp.bfloat16)
    q_full = jnp.concatenate([q_nope, q_rope], axis=1)
    key_nope = jnp.dot(normed, weight_head[:, :D_NOPE], preferred_element_type=jnp.float32).astype(jnp.bfloat16)
    value_rows = jnp.dot(normed, weight_head[:, D_NOPE:], preferred_element_type=jnp.float32).astype(jnp.bfloat16)
    key_full = jnp.concatenate([key_nope, key_rope], axis=1)
    scores = jnp.dot(q_full, key_full.T, preferred_element_type=jnp.float32) * score_scale
    scores = jnp.where(allowed, scores, masked_score)
    row_max = lax.optimization_barrier(jnp.max(scores, axis=1, keepdims=True))
    expo_rows = jnp.where(allowed, jnp.exp(scores - row_max), 0.0)
    prob_rows = expo_rows / lax.optimization_barrier(jnp.sum(expo_rows, axis=1, keepdims=True))
    prob_low = prob_rows.astype(jnp.bfloat16)
    output = jnp.dot(prob_low, value_rows, preferred_element_type=jnp.float32)
    delta_rows = lax.optimization_barrier(jnp.sum(out_head.astype(jnp.float32) * output, axis=1, keepdims=True))
    value_grad = jnp.dot(prob_low.T, out_head, preferred_element_type=jnp.float32).astype(jnp.bfloat16)
    prob_grad = jnp.dot(out_head, value_rows.T, preferred_element_type=jnp.float32)
    score_grad = (prob_rows * (prob_grad - delta_rows)).astype(jnp.bfloat16)
    key_grad = (jnp.dot(score_grad.T, q_nope, preferred_element_type=jnp.float32) * score_scale).astype(jnp.bfloat16)
    gradient = jnp.dot(normed.T, jnp.concatenate([key_grad, value_grad], axis=1), preferred_element_type=jnp.float32)
    return (output.astype(jnp.bfloat16), gradient)

def one_sequence(query_seq, latent_seq, seg_ids, grad_seq, up_weight, latent_gain):
    positions = doc_positions(seg_ids)
    normed = normalize(latent_seq, latent_gain)
    key_rope = rotate_pairs(latent_seq[:, D_LAT:].astype(jnp.float32), positions).astype(jnp.bfloat16)
    places = jnp.arange(SEQ_LEN, dtype=jnp.int32)
    allowed = (places[None, :] <= places[:, None]) & (seg_ids[None, :] == seg_ids[:, None])
    query_width = D_NOPE + D_ROPE
    pair_width = D_NOPE + D_VAL

    def per_head(head_index):
        query_head = lax.dynamic_slice_in_dim(query_seq, head_index * query_width, query_width, 1)
        out_head = lax.dynamic_slice_in_dim(grad_seq, head_index * D_VAL, D_VAL, 1)
        weight_head = lax.dynamic_slice_in_dim(up_weight, head_index * pair_width, pair_width, 1)
        return attend_head(query_head, out_head, normed, key_rope, weight_head, positions, allowed)
    outputs, gradients = lax.map(per_head, jnp.arange(HEADS, dtype=jnp.int32))
    attention = jnp.transpose(outputs, (1, 0, 2)).reshape(SEQ_LEN, HEADS * D_VAL)
    grad_all = jnp.transpose(gradients, (1, 0, 2)).reshape(D_LAT, HEADS * pair_width)
    return (attention, grad_all)

def reference(queries, latent, latent_gain, segments, up_weight, out_grad, hess_old):

    def per_seq(carry, index):
        attention, grad_all = one_sequence(queries[index], latent[index], segments[index], out_grad[index], up_weight, latent_gain)
        return (carry + grad_all, attention)
    start_total = jnp.zeros((D_LAT, HEADS * (D_NOPE + D_VAL)), jnp.float32)
    gradient, attn_out = lax.scan(per_seq, start_total, jnp.arange(BATCH, dtype=jnp.int32))
    hess_new = ema_decay * hess_old + (1.0 - ema_decay) * gradient * gradient
    return (attn_out, hess_new)
```

```python
import functools
import math

import jax
import jax.numpy as jnp
import numpy as np
from jax import lax
from jax.experimental import pallas as pl
from jax.experimental.pallas import tpu as pltpu
from jax.sharding import PartitionSpec as P

D_LAT = 512
D_ROPE = 64
D_NOPE = 128
D_VAL = 128
LANES = 128
PACK = D_LAT + LANES

epsilon = 1e-06
ema_decay = 0.99
rope_base = 10000.0
masked_score = -1e30
MESH = pl.DeviceIdType.MESH


def rope_table(reach):
    half = D_ROPE // 2
    steps_up = np.arange(half, dtype=np.float32)
    frequency = np.float32(rope_base) ** (-(np.float32(2.0) * steps_up) / np.float32(D_ROPE))
    angles = np.arange(reach, dtype=np.float32)[:, None] * frequency.astype(np.float32)[None, :]
    cosine = np.cos(angles.astype(np.float64)).astype(np.float32)
    sine = np.sin(angles.astype(np.float64)).astype(np.float32)
    whole = np.concatenate([cosine, cosine, -sine, sine], axis=1)
    parts = []
    for _ in range(3):
        part = whole.astype(jnp.bfloat16)
        parts.append(part)
        whole = whole - part.astype(np.float32)
    return np.stack(parts)


def swap_matrix():
    matrix = np.zeros((LANES, LANES), np.float32)
    for i in range(D_ROPE):
        matrix[i, i] = 1.0
        matrix[i, D_ROPE + (i + D_ROPE // 2) % D_ROPE] = 1.0
    return matrix.astype(jnp.bfloat16)


def mm(a, b):
    return jnp.dot(a, b, preferred_element_type=jnp.float32)


def mm_t(a, b):
    return lax.dot_general(a, b, (((1,), (1,)), ((), ())), preferred_element_type=jnp.float32)


def kernel(
    n,
    q_ref,
    lat_ref,
    gain_ref,
    seg_ref,
    w_ref,
    g_ref,
    table_ref,
    swap_ref,
    out_ref,
    grad_ref,
    buf,
    kfull,
    qfull,
    vals,
    vals_t,
    ends,
    g_t,
    q_t,
    acc,
    send_sem,
    recv_sem,
    fsend_sem,
    frecv_sem,
):
    me = lax.axis_index("seq")
    chips = n // 2
    chip = me // 2
    core = lax.rem(me, 2)
    sibling = chip * 2 + (1 - core)
    rows = lat_ref.shape[0]
    length = buf.shape[0]
    reach = table_ref.shape[1]

    def peer(step):
        return lax.rem(chip + step, chips) * 2 + core

    barrier = pltpu.get_barrier_semaphore()

    def greet(step, carry):
        pl.semaphore_signal(barrier, inc=1, device_id={"seq": peer(step)}, device_id_type=MESH)
        return carry

    lax.fori_loop(1, chips, greet, 0)
    pl.semaphore_signal(barrier, inc=1, device_id={"seq": sibling}, device_id_type=MESH)

    def block(owner):
        return buf.at[pl.ds(pl.multiple_of(owner * rows, rows), rows), :]

    compressed = lat_ref[:, :D_LAT].astype(jnp.float32)
    spread = jnp.mean(compressed * compressed, axis=-1, keepdims=True)
    normed = (compressed * lax.rsqrt(spread + epsilon) * gain_ref[...]).astype(jnp.bfloat16)
    mine = pl.ds(pl.multiple_of(me * rows, rows), rows)
    buf[mine, :D_LAT] = normed
    tail = jnp.concatenate(
        [
            lat_ref[:, D_LAT:],
            jnp.broadcast_to(seg_ref[...].astype(jnp.float32), (rows, LANES - D_ROPE)).astype(
                jnp.bfloat16
            ),
        ],
        axis=1,
    )
    buf[mine, D_LAT:] = tail

    pl.semaphore_wait(barrier, chips)

    def direct(step):
        return pltpu.make_async_remote_copy(
            src_ref=block(me),
            dst_ref=block(me),
            send_sem=send_sem.at[step],
            recv_sem=recv_sem.at[step],
            device_id={"seq": peer(step)},
            device_id_type=MESH,
        )

    def forward(step):
        owner = lax.rem(chip + chips - step, chips) * 2 + core
        return pltpu.make_async_remote_copy(
            src_ref=block(owner),
            dst_ref=block(owner),
            send_sem=fsend_sem.at[step],
            recv_sem=frecv_sem.at[step],
            device_id={"seq": sibling},
            device_id_type=MESH,
        )

    def launch(step, carry):
        direct(step).start()
        return carry

    lax.fori_loop(1, chips, launch, 0)
    forward(0).start()

    g_t[...] = g_ref[...].astype(jnp.float32).T.astype(jnp.bfloat16)
    q_t[...] = q_ref[:, :D_NOPE].astype(jnp.float32).T.astype(jnp.bfloat16)
    weight_v_t = w_ref[:, D_NOPE:].astype(jnp.float32).T.astype(jnp.bfloat16)

    def relay(step, carry):
        direct(step).wait_recv()
        forward(step).start()
        return carry

    lax.fori_loop(1, chips, relay, 0)

    def arrive(step, carry):
        forward(step).wait_recv()
        return carry

    lax.fori_loop(0, chips, arrive, 0)

    lane_seg = buf[:, D_LAT:].astype(jnp.float32)
    spare = pltpu.roll(lane_seg, D_ROPE, 1)
    lane = lax.broadcasted_iota(jnp.int32, (length, LANES), 1)
    seg_all = jnp.where(lane < D_ROPE, spare, lane_seg)
    lane_f = lane.astype(jnp.float32)
    before = jnp.sum(jnp.where(seg_all < lane_f, 1.0, 0.0), axis=0, keepdims=True)
    within = jnp.sum(jnp.where(seg_all <= lane_f, 1.0, 0.0), axis=0, keepdims=True)
    counts = jnp.concatenate(
        [
            jnp.broadcast_to(before, (LANES, LANES)).T,
            jnp.broadcast_to(within, (LANES, LANES)).T,
        ],
        axis=1,
    )
    high = jnp.floor(counts * (1.0 / 256.0)) * 256.0
    low = (counts - high).astype(jnp.bfloat16)
    high = high.astype(jnp.bfloat16)
    member = jnp.where(seg_all == lane_f, 1.0, 0.0).astype(jnp.bfloat16)
    bounds = mm(member, high) + mm(member, low)
    ends[...] = bounds[:, LANES:]
    token = lax.broadcasted_iota(jnp.int32, (length, LANES), 0).astype(jnp.float32)
    position = token - bounds[:, :LANES]
    columns = []
    for base in range(0, reach, LANES):
        columns.append(jnp.where(position == lane_f + float(base), 1.0, 0.0).astype(jnp.bfloat16))
    spot = jnp.concatenate(columns, axis=1)
    turn = mm(spot, table_ref[0]) + mm(spot, table_ref[1]) + mm(spot, table_ref[2])

    def rotate(pair):
        product = pair * turn
        return product + pltpu.roll(product, D_ROPE, 1)

    keep = lane < D_ROPE
    kfull[:, D_NOPE:] = rotate(mm(buf[:, D_LAT:], swap_ref[...])).astype(jnp.bfloat16)
    qfull[:, :D_NOPE] = q_ref[:, :D_NOPE]
    q_pair = mm(q_ref[:, D_NOPE:], swap_ref[:D_ROPE, :])
    qfull[:, D_NOPE:] = jnp.where(keep, rotate(q_pair), 0.0).astype(jnp.bfloat16)

    projected = mm(buf[:, :D_LAT], w_ref[...])
    kfull[:, :D_NOPE] = projected[:, :D_NOPE].astype(jnp.bfloat16)
    vals[...] = projected[:, D_NOPE:].astype(jnp.bfloat16)
    vals_t[...] = mm_t(weight_v_t, buf[:, :D_LAT]).astype(jnp.bfloat16)

    score_scale = (D_NOPE + D_ROPE) ** (-0.5)
    exponent_scale = score_scale * math.log2(math.e)
    acc[...] = jnp.zeros_like(acc)
    step_rows = LANES
    for lower in range(0, length, step_rows):
        upper = lower + step_rows
        first = max(0, lower - (reach - 1)) // LANES * LANES
        span = upper - first
        scores = mm_t(kfull[first:upper, :], qfull[lower:upper, :])
        key_at = lax.broadcasted_iota(jnp.int32, (span, step_rows), 0) + first
        query_at = lax.broadcasted_iota(jnp.int32, (span, step_rows), 1) + lower
        allowed = (query_at >= key_at) & (query_at.astype(jnp.float32) < ends[first:upper, :])
        scores = jnp.where(allowed, scores, masked_score)
        top = jnp.max(scores, axis=0, keepdims=True)
        expo = jnp.exp2((scores - top) * exponent_scale)
        total = jnp.sum(expo, axis=0, keepdims=True)
        prob = expo * (1.0 / total)
        prob_low = prob.astype(jnp.bfloat16)
        prob_grad = mm_t(vals[first:upper, :], g_ref[lower:upper, :])
        delta = jnp.sum(prob_low.astype(jnp.float32) * prob_grad, axis=0, keepdims=True)
        score_grad = (prob * (prob_grad - delta)).astype(jnp.bfloat16)
        output_t = mm(vals_t[:, first:upper], prob_low)
        out_ref[lower:upper, :] = output_t.T.astype(jnp.bfloat16)
        acc[:D_NOPE, first:upper] += mm_t(q_t[:, lower:upper], score_grad)
        acc[D_NOPE:, first:upper] += mm_t(g_t[:, lower:upper], prob_low)

    key_low = (acc[:D_NOPE, :] * score_scale).astype(jnp.bfloat16)
    value_low = acc[D_NOPE:, :].astype(jnp.bfloat16)
    columns_t = jnp.concatenate([key_low, value_low], axis=0)
    grad_ref[...] = mm(columns_t, buf[:, :D_LAT]).T

    def drain(step, carry):
        direct(step).wait_send()
        forward(step).wait_send()
        return carry

    forward(0).wait_send()
    lax.fori_loop(1, chips, drain, 0)


def local(n, copies, queries, latent, latent_gain, segments, up_weight, out_grad, hess_old):
    weight = up_weight
    if copies > 1:
        weight = lax.all_gather(up_weight, "dp", axis=0, tiled=True)
    length = queries.shape[1]
    reach = length // 4
    chips = n // 2
    table = jnp.asarray(rope_table(reach))
    swap = jnp.asarray(swap_matrix())
    vmem = pl.BlockSpec(memory_space=pltpu.VMEM)
    attn, gradient = pl.pallas_call(
        functools.partial(kernel, n),
        out_shape=(
            jax.ShapeDtypeStruct((length, D_VAL), jnp.bfloat16),
            jax.ShapeDtypeStruct((D_LAT, D_NOPE + D_VAL), jnp.float32),
        ),
        in_specs=[vmem] * 8,
        out_specs=(vmem, vmem),
        scratch_shapes=[
            pltpu.VMEM((length, PACK), jnp.bfloat16),
            pltpu.VMEM((length, 2 * LANES), jnp.bfloat16),
            pltpu.VMEM((length, 2 * LANES), jnp.bfloat16),
            pltpu.VMEM((length, D_VAL), jnp.bfloat16),
            pltpu.VMEM((D_VAL, length), jnp.bfloat16),
            pltpu.VMEM((length, LANES), jnp.float32),
            pltpu.VMEM((D_VAL, length), jnp.bfloat16),
            pltpu.VMEM((D_NOPE, length), jnp.bfloat16),
            pltpu.VMEM((D_NOPE + D_VAL, length), jnp.float32),
            pltpu.SemaphoreType.DMA((chips,)),
            pltpu.SemaphoreType.DMA((chips,)),
            pltpu.SemaphoreType.DMA((chips,)),
            pltpu.SemaphoreType.DMA((chips,)),
        ],
        compiler_params=pltpu.CompilerParams(
            collective_id=0, has_side_effects=True, vmem_limit_bytes=48 << 20
        ),
    )(
        queries[0],
        latent[0],
        latent_gain[None, :],
        segments[0][:, None],
        weight,
        out_grad[0],
        table,
        swap,
    )
    if copies > 1:
        gradient = lax.psum_scatter(gradient, "dp", scatter_dimension=0, tiled=True)
    hess_new = ema_decay * hess_old + (1.0 - ema_decay) * gradient * gradient
    return (attn[None], hess_new)


def solution(mesh):
    return jax.shard_map(
        functools.partial(local, mesh.shape["seq"], mesh.shape["dp"]),
        mesh=mesh,
        in_specs=(
            P("dp", None, "seq"),
            P("dp", "seq", None),
            P(),
            P("dp", "seq"),
            P("dp", "seq"),
            P("dp", None, "seq"),
            P("dp", "seq"),
        ),
        out_specs=(P("dp", None, "seq"), P("dp", "seq")),
        check_vma=False,
    )
```

```python
import functools
import math

import jax
import jax.numpy as jnp
import numpy as np
from jax import lax
from jax.experimental import pallas as pl
from jax.experimental.pallas import tpu as pltpu
from jax.sharding import PartitionSpec as P

D_LAT = 512
D_ROPE = 64
D_NOPE = 128
D_VAL = 128
LANES = 128
PACK = D_LAT + LANES
SIDE = 2

epsilon = 1e-06
ema_decay = 0.99
rope_base = 10000.0
masked_score = -1e30
MESH = pl.DeviceIdType.MESH


def rope_table(reach):
    half = D_ROPE // 2
    steps_up = np.arange(half, dtype=np.float32)
    frequency = np.float32(rope_base) ** (-(np.float32(2.0) * steps_up) / np.float32(D_ROPE))
    angles = np.arange(reach, dtype=np.float32)[:, None] * frequency.astype(np.float32)[None, :]
    cosine = np.cos(angles.astype(np.float64)).astype(np.float32)
    sine = np.sin(angles.astype(np.float64)).astype(np.float32)
    whole = np.concatenate([cosine, cosine, -sine, sine], axis=1)
    parts = []
    for _ in range(3):
        part = whole.astype(jnp.bfloat16)
        parts.append(part)
        whole = whole - part.astype(np.float32)
    return np.stack(parts)


def swap_matrix(shape, dim):
    entry = lax.broadcasted_iota(jnp.int32, shape, dim)
    place = lax.broadcasted_iota(jnp.int32, shape, 1 - dim)
    half = D_ROPE // 2
    partner = D_ROPE + jnp.where(entry < half, entry + half, entry - half)
    hit = (entry < D_ROPE) & ((place == entry) | (place == partner))
    return jnp.where(hit, 1.0, 0.0).astype(jnp.bfloat16)


def mm(a, b):
    return jnp.dot(a, b, preferred_element_type=jnp.float32)


def mm_t(a, b):
    return lax.dot_general(a, b, (((1,), (1,)), ((), ())), preferred_element_type=jnp.float32)


def kernel(
    n,
    q_hbm,
    lat_hbm,
    gain_hbm,
    seg_hbm,
    w_hbm,
    g_hbm,
    table_hbm,
    out_ref,
    grad_ref,
    q_ref,
    lat_ref,
    gain_ref,
    seg_ref,
    w_ref,
    g_ref,
    table_ref,
    buf,
    kfull,
    qfull_t,
    vals,
    vals_t,
    ends,
    g_t,
    weight_v_t,
    acc,
    send_sem,
    recv_sem,
    load_sem,
):
    me = lax.axis_index("seq")
    chip = me // 2
    core = lax.rem(me, 2)
    minor = lax.rem(chip, SIDE * SIDE)
    major = chip // (SIDE * SIDE)
    planes = n // (2 * SIDE * SIDE)
    minor_x = minor + 1 - 2 * lax.rem(minor, SIDE)
    minor_y = minor + SIDE - 2 * SIDE * (minor // SIDE)
    minor_d = minor_x + minor_y - minor

    def device(plane, place, side):
        return (plane * (SIDE * SIDE) + place) * 2 + side

    def plane_of(step):
        return lax.rem(major + planes + step, planes)

    sibling = device(major, minor, 1 - core)
    across_x = device(major, minor_x, core)
    across_y = device(major, minor_y, core)
    across_d = device(major, minor_d, core)
    partners = [sibling, across_x, across_y, across_d]
    partners += [device(plane_of(step), minor, core) for step in range(1, planes)]
    rows = lat_ref.shape[0]
    length = buf.shape[0]
    reach = table_ref.shape[1]

    pairs = (
        (lat_hbm, lat_ref),
        (gain_hbm, gain_ref),
        (seg_hbm, seg_ref),
        (g_hbm, g_ref),
        (w_hbm, w_ref),
        (q_hbm, q_ref),
        (table_hbm, table_ref),
    )
    loads = [
        pltpu.make_async_copy(source, target, load_sem.at[at])
        for at, (source, target) in enumerate(pairs)
    ]
    for load in loads[:3]:
        load.start()
    barrier = pltpu.get_barrier_semaphore()
    for partner in partners:
        pl.semaphore_signal(barrier, inc=1, device_id={"seq": partner}, device_id_type=MESH)

    def block(owner):
        return buf.at[pl.ds(pl.multiple_of(owner * rows, rows), rows), :]

    for load in loads[3:]:
        load.start()
    for load in loads[:3]:
        load.wait()
    compressed = lat_ref[:, :D_LAT].astype(jnp.float32)
    spread = jnp.mean(compressed * compressed, axis=-1, keepdims=True)
    normed = (compressed * lax.rsqrt(spread + epsilon) * gain_ref[...]).astype(jnp.bfloat16)
    mine = pl.ds(pl.multiple_of(me * rows, rows), rows)
    buf[mine, :D_LAT] = normed
    down = lax.broadcasted_iota(jnp.int32, (rows, rows), 0)
    right = lax.broadcasted_iota(jnp.int32, (rows, rows), 1)
    seg_column = jnp.sum(
        jnp.where(down == right, seg_ref[...].astype(jnp.float32), 0.0), axis=1, keepdims=True
    )
    seg_wide = jnp.broadcast_to(seg_column, (rows, LANES - D_ROPE)).astype(jnp.bfloat16)
    tail = jnp.concatenate([lat_ref[:, D_LAT:], seg_wide], axis=1)
    buf[mine, D_LAT:] = tail

    pl.semaphore_wait(barrier, len(partners))

    def send(owner, slot, target):
        return pltpu.make_async_remote_copy(
            src_ref=block(owner),
            dst_ref=block(owner),
            send_sem=send_sem.at[slot],
            recv_sem=recv_sem.at[slot],
            device_id={"seq": target},
            device_id_type=MESH,
        )

    places = (minor, minor_x, minor_y, minor_d)

    def along(step):
        return send(me, 8 * step, device(plane_of(step), minor, core))

    def over(way, step):
        owner = device(plane_of(-step), minor, core)
        return send(owner, 8 * step + 1 + way, (across_x, across_y, across_d)[way])

    def share(place, step):
        owner = device(plane_of(-step), places[place], core)
        return send(owner, 8 * step + 4 + place, sibling)

    started = []

    def begin(copy):
        copy.start()
        started.append(copy)

    order = sorted(range(1, planes), key=lambda step: (min(step, planes - step), step))
    for step in order:
        begin(along(step))
    for way in range(3):
        begin(over(way, 0))
    begin(share(0, 0))

    for load in loads[3:]:
        load.wait()
    g_t[...] = g_ref[...].astype(jnp.float32).T.astype(jnp.bfloat16)
    weight_v_t[...] = w_ref[:, D_NOPE:].astype(jnp.float32).T.astype(jnp.bfloat16)
    swap = swap_matrix((LANES, LANES), 0)
    swap_t = swap_matrix((LANES, D_ROPE), 1)
    qfull_t[:D_NOPE, :] = q_ref[:D_NOPE, :]
    qfull_t[D_NOPE + D_ROPE :, :] = jnp.zeros_like(qfull_t[D_NOPE + D_ROPE :, :])

    def crossed(step):
        for way in range(3):
            over(way, step).wait_recv()
            begin(share(1 + way, step))

    for step in order:
        along(step).wait_recv()
        for way in range(3):
            begin(over(way, step))
        begin(share(0, step))
        if step == order[0]:
            crossed(0)
    for step in order:
        crossed(step)

    plane_rows = 2 * SIDE * SIDE * rows
    for step in [0] + order:
        for place in range(4):
            share(place, step).wait_recv()
        here = pl.ds(pl.multiple_of(plane_of(-step) * plane_rows, plane_rows), plane_rows)
        arrived = buf[here, :D_LAT]
        projected = mm(arrived, w_ref[...])
        kfull[here, :D_NOPE] = projected[:, :D_NOPE].astype(jnp.bfloat16)
        vals[here, :] = projected[:, D_NOPE:].astype(jnp.bfloat16)
        vals_t[:, here] = mm_t(weight_v_t[...], arrived).astype(jnp.bfloat16)

    lane_seg = buf[:, D_LAT:].astype(jnp.float32)
    spare = pltpu.roll(lane_seg, D_ROPE, 1)
    lane = lax.broadcasted_iota(jnp.int32, (length, LANES), 1)
    seg_all = jnp.where(lane < D_ROPE, spare, lane_seg)
    lane_f = lane.astype(jnp.float32)
    before = jnp.sum(jnp.where(seg_all < lane_f, 1.0, 0.0), axis=0, keepdims=True)
    within = jnp.sum(jnp.where(seg_all <= lane_f, 1.0, 0.0), axis=0, keepdims=True)
    counts = jnp.concatenate(
        [
            jnp.broadcast_to(before, (LANES, LANES)).T,
            jnp.broadcast_to(within, (LANES, LANES)).T,
        ],
        axis=1,
    )
    high = jnp.floor(counts * (1.0 / 256.0)) * 256.0
    low = (counts - high).astype(jnp.bfloat16)
    high = high.astype(jnp.bfloat16)
    member = jnp.where(seg_all == lane_f, 1.0, 0.0).astype(jnp.bfloat16)
    bounds = mm(member, high) + mm(member, low)
    ends[...] = bounds[:, LANES:]
    token = lax.broadcasted_iota(jnp.int32, (length, LANES), 0).astype(jnp.float32)
    position = token - bounds[:, :LANES]
    columns = []
    for base in range(0, reach, LANES):
        columns.append(jnp.where(position == lane_f + float(base), 1.0, 0.0).astype(jnp.bfloat16))
    spot = jnp.concatenate(columns, axis=1)
    turn = mm(spot, table_ref[0]) + mm(spot, table_ref[1]) + mm(spot, table_ref[2])

    product = mm(buf[:, D_LAT:], swap) * turn
    kfull[:, D_NOPE:] = (product + pltpu.roll(product, D_ROPE, 1)).astype(jnp.bfloat16)
    product_t = mm(swap_t, q_ref[D_NOPE:, :]) * turn.T
    qfull_t[D_NOPE : D_NOPE + D_ROPE, :] = (product_t[:D_ROPE, :] + product_t[D_ROPE:, :]).astype(
        jnp.bfloat16
    )

    score_scale = (D_NOPE + D_ROPE) ** (-0.5)
    exponent_scale = score_scale * math.log2(math.e)
    acc[...] = jnp.zeros_like(acc)
    step_rows = LANES
    for lower in range(0, length, step_rows):
        upper = lower + step_rows
        first = max(0, lower - (reach - 1)) // LANES * LANES
        span = upper - first
        scores = mm(kfull[first:upper, :], qfull_t[:, lower:upper])
        key_at = lax.broadcasted_iota(jnp.int32, (span, step_rows), 0) + first
        query_at = lax.broadcasted_iota(jnp.int32, (span, step_rows), 1) + lower
        allowed = (query_at >= key_at) & (query_at.astype(jnp.float32) < ends[first:upper, :])
        scores = jnp.where(allowed, scores, masked_score)
        top = jnp.max(scores, axis=0, keepdims=True)
        expo = jnp.exp2((scores - top) * exponent_scale)
        total = jnp.sum(expo, axis=0, keepdims=True)
        prob = expo * (1.0 / total)
        prob_low = prob.astype(jnp.bfloat16)
        prob_grad = mm_t(vals[first:upper, :], g_ref[lower:upper, :])
        delta = jnp.sum(prob_low.astype(jnp.float32) * prob_grad, axis=0, keepdims=True)
        score_grad = (prob * (prob_grad - delta)).astype(jnp.bfloat16)
        output_t = mm(vals_t[:, first:upper], prob_low)
        out_ref[lower:upper, :] = output_t.T.astype(jnp.bfloat16)
        acc[:D_NOPE, first:upper] += mm_t(q_ref[:D_NOPE, lower:upper], score_grad)
        acc[D_NOPE:, first:upper] += mm_t(g_t[:, lower:upper], prob_low)

    key_low = (acc[:D_NOPE, :] * score_scale).astype(jnp.bfloat16)
    value_low = acc[D_NOPE:, :].astype(jnp.bfloat16)
    columns_t = jnp.concatenate([key_low, value_low], axis=0)
    grad_ref[...] = mm(columns_t, buf[:, :D_LAT]).T

    for copy in started:
        copy.wait_send()


def local(n, copies, queries, latent, latent_gain, segments, up_weight, out_grad, hess_old):
    weight = up_weight
    if copies > 1:
        weight = lax.all_gather(up_weight, "dp", axis=0, tiled=True)
    length = queries.shape[1]
    reach = length // 4
    slots = 8 * (n // (2 * SIDE * SIDE))
    table = jnp.asarray(rope_table(reach))
    operands = (
        queries[0].T,
        latent[0],
        latent_gain[None, :],
        segments,
        weight,
        out_grad[0],
        table,
    )
    vmem = pl.BlockSpec(memory_space=pltpu.VMEM)
    attn, gradient = pl.pallas_call(
        functools.partial(kernel, n),
        out_shape=(
            jax.ShapeDtypeStruct((length, D_VAL), jnp.bfloat16),
            jax.ShapeDtypeStruct((D_LAT, D_NOPE + D_VAL), jnp.float32),
        ),
        in_specs=[pl.BlockSpec(memory_space=pltpu.HBM)] * len(operands),
        out_specs=(vmem, vmem),
        scratch_shapes=[pltpu.VMEM(operand.shape, operand.dtype) for operand in operands]
        + [
            pltpu.VMEM((length, PACK), jnp.bfloat16),
            pltpu.VMEM((length, 2 * LANES), jnp.bfloat16),
            pltpu.VMEM((2 * LANES, length), jnp.bfloat16),
            pltpu.VMEM((length, D_VAL), jnp.bfloat16),
            pltpu.VMEM((D_VAL, length), jnp.bfloat16),
            pltpu.VMEM((length, LANES), jnp.float32),
            pltpu.VMEM((D_VAL, length), jnp.bfloat16),
            pltpu.VMEM((D_VAL, D_LAT), jnp.bfloat16),
            pltpu.VMEM((D_NOPE + D_VAL, length), jnp.float32),
            pltpu.SemaphoreType.DMA((slots,)),
            pltpu.SemaphoreType.DMA((slots,)),
            pltpu.SemaphoreType.DMA((len(operands),)),
        ],
        compiler_params=pltpu.CompilerParams(
            collective_id=0, has_side_effects=True
        ),
    )(*operands)
    if copies > 1:
        gradient = lax.psum_scatter(gradient, "dp", scatter_dimension=0, tiled=True)
    hess_new = ema_decay * hess_old + (1.0 - ema_decay) * gradient * gradient
    return (attn[None], hess_new)


def solution(mesh):
    return jax.shard_map(
        functools.partial(local, mesh.shape["seq"], mesh.shape["dp"]),
        mesh=mesh,
        in_specs=(
            P("dp", None, "seq"),
            P("dp", "seq", None),
            P(),
            P("dp", "seq"),
            P("dp", "seq"),
            P("dp", None, "seq"),
            P("dp", "seq"),
        ),
        out_specs=(P("dp", None, "seq"), P("dp", "seq")),
        check_vma=False,
    )
```
